32 devices in a mesh: groups: 2 (over x), frames: 8 (over z, y), heads: 2 (over core).
Axes of the slice: x: 2, y: 2, z: 4, core: 2. Of those that a mesh axis runs over, the one named last changes fastest.
Arguments:
- query_main: bfloat16 [6144, 1536], P(('groups', 'frames', 'heads')), parts along dimension 0, may hold values from -5.5 to 5.5
- key_main: bfloat16 [6144, 1536], P(('groups', 'frames', 'heads')), parts along dimension 0, may hold values from -5.5 to 5.5
- value_main: bfloat16 [6144, 1536], P(('groups', 'frames', 'heads')), parts along dimension 0, may hold values from -6 to 6
- query_tangent: bfloat16 [6144, 1536], P(('groups', 'frames', 'heads')), parts along dimension 0, may hold values from -6 to 6
- key_tangent: bfloat16 [6144, 1536], P(('groups', 'frames', 'heads')), parts along dimension 0, may hold values from -6 to 6
- value_tangent: bfloat16 [6144, 1536], P(('groups', 'frames', 'heads')), parts along dimension 0, may hold values from -6 to 6
- target: bfloat16 [6144, 1536], P(('groups', 'frames'), 'heads'), parts along dimension 0, may hold values from -3 to 3
Outputs:
- query_grad: bfloat16 [6144, 1536], P(('groups', 'frames'), 'heads'), parts along dimension 0
- key_grad: bfloat16 [6144, 1536], P(('groups', 'frames'), 'heads'), parts along dimension 0
- value_grad: bfloat16 [6144, 1536], P(('groups', 'frames'), 'heads'), parts along dimension 0
The draws below stay inside these ranges and needn't reach their ends.
There are 2 independent parts, one for each index of `groups`. The reference program is written for one: setup_inputs(seed, part) draws one part's arguments, and reference() takes and returns one part's arrays. A program takes and returns all parts, laid end to end along the dimension named above; each array names one. Nothing has to cross between parts.
All inputs are finite; a program needn't handle non-finite values.
Results may differ from the reference program's by a relative error of at most 0.0071.
Values may be sent and summed in bfloat16 or wider, within the bound.
No kernel may reach another device: no remote copies, remote signals or barrier semaphores. Data moves between devices by JAX's collectives and lax.ppermute only.
A program may use at most 64 MiB of HBM per device.

```python
import jax
import jax.numpy as jnp
from jax import lax

HEADS = 24
HD = 64
D = 1536
SLAB = 768
TOKENS = 3072


def draw_query_main(key, part):
    values_drawn = jnp.clip(1.25 * jax.random.normal(jax.random.fold_in(key, 1), (TOKENS, D), jnp.float32), -5.5, 5.5)
    return values_drawn.astype(jnp.bfloat16)


def draw_key_main(key, part):
    values_drawn = jnp.clip(1.25 * jax.random.normal(jax.random.fold_in(key, 2), (TOKENS, D), jnp.float32), -5.5, 5.5)
    return values_drawn.astype(jnp.bfloat16)


def level_of(key, extent, cuts, least, top_value):
    def one(dim, parts):
        steps = jax.random.uniform(jax.random.fold_in(jax.random.fold_in(key, 6), dim), (parts,), jnp.float32, least / len(cuts), top_value / len(cuts))
        return jnp.repeat(jnp.exp(steps), extent[dim] // parts).reshape((-1,) + (1,) * (len(extent) - dim - 1))

    loudness = one(*cuts[0])
    for cut in cuts[1:]:
        loudness = loudness * one(*cut)
    return loudness


def bell_draw(stream_key, dims, spread, bound, shards=(), kind=jnp.bfloat16):
    values = jax.random.normal(stream_key, dims, jnp.float32) * spread
    if len(shards) > 0:
        values = level_of(stream_key, dims, shards, -0.22, 0.18) * values
    return jnp.clip(values, min=-bound, max=bound).astype(kind)


def setup_inputs(seed: int = 0, part: int = 0) -> dict:
    streams_of = jax.random.split(jax.random.key(seed), 8)
    own_keys = jax.random.split(jax.random.fold_in(streams_of[7], part), 8)
    return {
        "query_main": draw_query_main(jax.random.fold_in(jax.random.fold_in(streams_of[7], part), 71), part),
        "key_main": draw_key_main(jax.random.fold_in(jax.random.fold_in(streams_of[7], part), 71), part),
        "value_main": bell_draw(own_keys[2], (TOKENS, D), 1.0, 6.0, ((0, 16),)),
        "query_tangent": bell_draw(own_keys[3], (TOKENS, D), 1.0, 6.0, ((0, 16),)),
        "key_tangent": bell_draw(own_keys[4], (TOKENS, D), 1.0, 6.0, ((0, 16),)),
        "value_tangent": bell_draw(own_keys[5], (TOKENS, D), 1.0, 6.0, ((0, 16),)),
        "target": bell_draw(own_keys[6], (TOKENS, D), 0.5, 3.0, ((0, 8), (1, 2))),
    }


def lowered(array):
    return lax.optimization_barrier(array.astype(jnp.bfloat16)).astype(jnp.float32)


def product(form, left, right):
    return jnp.einsum(form, left, right, precision=lax.Precision.HIGHEST)


def attend(queries, qtangent, key_rows, value_rows, ktangent, vtangent, goal, visible):
    score_scale = 1.0 / (HD ** 0.5)
    scores = product('qhd,khd->hqk', queries, key_rows) * score_scale
    scores = jnp.where(visible[None, None, :], scores, -jnp.inf)
    row_max = jnp.max(scores, axis=-1, keepdims=True)
    log_total = row_max + jnp.log(jnp.sum(jnp.exp(scores - row_max), axis=-1, keepdims=True))
    weights = jnp.exp(scores - log_total)
    weights_low = lowered(weights)
    tangent_scores = (product('qhd,khd->hqk', qtangent, key_rows) + product('qhd,khd->hqk', queries, ktangent)) * score_scale
    tangent_weights = weights * (tangent_scores - jnp.sum(weights * tangent_scores, axis=-1, keepdims=True))
    tangent_low = lowered(tangent_weights)
    primal_out = product('hqk,khd->qhd', weights_low, value_rows)
    tangent_out = product('hqk,khd->qhd', tangent_low, value_rows) + product('hqk,khd->qhd', weights_low, vtangent)
    residual_grad = lowered(2.0 * (primal_out - goal - tangent_out))
    score_grad = product('qhd,khd->hqk', residual_grad, value_rows)
    delta = jnp.sum(weights * score_grad, axis=-1, keepdims=True)
    score_low = lowered(weights * (score_grad - delta))
    query_grad = product('hqk,khd->qhd', score_low, key_rows) * score_scale
    key_grad = product('hqk,qhd->khd', score_low, queries) * score_scale
    value_grad = product('hqk,qhd->khd', weights_low, residual_grad)
    return query_grad, key_grad, value_grad


def reference(query_main, key_main, value_main, query_tangent, key_tangent, value_tangent, target):
    count = TOKENS // SLAB

    def split(array):
        return array.astype(jnp.float32).reshape(count, SLAB, HEADS, HD)

    queries, key_rows, value_rows, qtangent, ktangent, vtangent, goal = [split(a) for a in (query_main, key_main, value_main, query_tangent, key_tangent, value_tangent, target)]

    def one_slab(slab_index):
        def current(array):
            return lax.dynamic_index_in_dim(array, slab_index, 0, keepdims=False)

        def window(array):
            earlier = lax.dynamic_index_in_dim(array, jnp.maximum(slab_index - 1, 0), 0, keepdims=False)
            earlier = jnp.where(slab_index > 0, earlier, jnp.zeros_like(earlier))
            return jnp.concatenate((earlier, current(array)), axis=0)

        visible = (jnp.arange(2 * SLAB) >= SLAB) | (slab_index > 0)
        return attend(current(queries), current(qtangent), window(key_rows), window(value_rows), window(ktangent), window(vtangent), current(goal), visible)

    query_grad, key_part, value_part = lax.map(one_slab, jnp.arange(count, dtype=jnp.int32))

    def combine(part):
        later = jnp.concatenate((part[1:, :SLAB], jnp.zeros_like(part[:1, :SLAB])), axis=0)
        return part[:, SLAB:] + later

    def finish(array):
        return array.reshape(TOKENS, D).astype(jnp.bfloat16)

    return finish(query_grad), finish(combine(key_part)), finish(combine(value_part))
```

```python
import functools
import math

import jax
import jax.numpy as jnp
from jax import lax
from jax.experimental import pallas as pl
from jax.experimental.pallas import tpu as pltpu
from jax.sharding import PartitionSpec as P

HD = 64
SLAB = 768
LANES = 128
BF16 = jnp.bfloat16
F32 = jnp.float32


def dot(left, right):
    return lax.dot_general(left, right, (((1,), (0,)), ((), ())), preferred_element_type=F32)


def dot_nt(left, right):
    return lax.dot_general(left, right, (((1,), (1,)), ((), ())), preferred_element_type=F32)


def run_copies(copies):
    for copy in copies:
        copy.start()
    for copy in copies:
        copy.wait()


def core_pack_kernel(chunks, *refs):
    sources, sends, sems = refs[:6], refs[6:-1], refs[-1]
    core = lax.axis_index("heads")
    half = sources[0].shape[1] // 2
    quarter = half // 2
    copies = []
    for chunk in range(chunks):
        for side in range(2):
            offset = pl.multiple_of((1 - core) * half + (side * quarter + chunk * LANES), LANES)
            for i, source in enumerate(sources):
                copies.append(
                    pltpu.make_async_copy(
                        source.at[:, pl.ds(offset, LANES)],
                        sends[chunk].at[side, i],
                        sems.at[len(copies)],
                    )
                )
    run_copies(copies)


def frame_pack_kernel(chunk, *refs):
    sources, target, got = refs[:6], refs[6], refs[7]
    kv_mine, kv_send, q_mine, q_send, sems = refs[8:]
    core = lax.axis_index("heads")
    parity = lax.rem(lax.axis_index("frames"), 2)
    rows, width = sources[0].shape
    half = width // 2
    quarter = half // 2
    copies = []

    def add(source, place):
        copies.append(pltpu.make_async_copy(source, place, sems.at[len(copies)]))

    for send in range(2):
        side = 1 - parity if send else parity
        kv_out = kv_send if send else kv_mine
        q_out = q_send if send else q_mine
        column = pl.multiple_of(side * quarter + chunk * LANES, LANES)
        offset = pl.multiple_of(core * half + side * quarter + chunk * LANES, LANES)
        own_rows = pl.ds(pl.multiple_of(core * rows, rows), rows)
        other_rows = pl.ds(pl.multiple_of((1 - core) * rows, rows), rows)
        for i in range(6):
            out, j = (kv_out, i) if i < 4 else (q_out, i - 4)
            add(sources[i].at[:, pl.ds(offset, LANES)], out.at[j, own_rows])
            add(got.at[side, i], out.at[j, other_rows])
        add(target.at[:, pl.ds(column, LANES)], q_out.at[2])
    run_copies(copies)


def attend_kernel(
    qb, kb, flag_ref,
    q_mine, q_part, kv_mine, kv_part, kz_mine, kz_part,
    dq_mine, dq_part, own_out, back_out,
    q_s, v_s, kkt_s, kT_s, vvT_s, s_s, ts_s, p_s, dq_s, dk_s, dv_s,
):
    half = q_mine.shape[1]
    slab = 2 * half
    own_chunks = slab // kb
    chunks = 2 * own_chunks
    step = pl.program_id(0)
    scale = 1.0 / math.sqrt(HD)

    @pl.when(step == 0)
    def _():
        for part, source in enumerate((q_mine, q_part)):
            rows = pl.ds(part * half, half)
            q_s[0, rows] = source[0] * jnp.asarray(scale, BF16)
            q_s[1, rows] = source[1] * jnp.asarray(scale, BF16)
            q_s[2, rows] = source[2]
        for part, source in enumerate((kv_mine, kv_part, kz_mine, kz_part)):
            rows = pl.ds(part * half, half)
            kkt_s[rows, :LANES] = source[0]
            kkt_s[rows, LANES:] = source[2]
            v_s[rows] = source[1]
            kT_s[:, rows] = source[0].T
            value_t = source[1].T
            vtangent_t = source[3].T
            for h in range(2):
                vvT_s[2 * HD * h : 2 * HD * h + HD, rows] = value_t[HD * h : HD * h + HD]
                vvT_s[2 * HD * h + HD : 2 * HD * (h + 1), rows] = vtangent_t[HD * h : HD * h + HD]
        dk_s[...] = jnp.zeros_like(dk_s)
        dv_s[...] = jnp.zeros_like(dv_s)

    lane = lax.broadcasted_iota(jnp.int32, (qb, LANES), 1)
    hide = (1.0 - flag_ref[0].astype(F32)) * 1e30
    qrows = pl.ds(pl.multiple_of(step * qb, qb), qb)
    queries = q_s[0, qrows]
    qtangent = q_s[1, qrows]
    goal_t = q_s[2, qrows].astype(F32).T
    state = [{}, {}]
    dq_parts = []

    def score_pass(h):
        keep = (lane // HD) == h
        q_masked = jnp.where(keep, queries, jnp.zeros_like(queries))
        qt_masked = jnp.where(keep, qtangent, jnp.zeros_like(qtangent))
        both = jnp.concatenate((qt_masked, q_masked), axis=1)
        peaks = [None, None]
        for c in range(chunks):
            rows = pl.ds(c * kb, kb)
            scores = dot_nt(kkt_s[rows, :LANES], q_masked)
            s_s[h, rows] = scores
            ts_s[h, rows] = dot_nt(kkt_s[rows], both)
            peak = jnp.max(scores, axis=0, keepdims=True)
            e = c // own_chunks
            peaks[e] = peak if peaks[e] is None else jnp.maximum(peaks[e], peak)
        peak = jnp.maximum(peaks[0], peaks[1] - hide)
        state[h].update(q=q_masked, peak=(peak, peak + hide))

    def weight_pass(h):
        total = mean = acc = 0.0
        for c in range(chunks):
            rows = pl.ds(c * kb, kb)
            e = jnp.exp(s_s[h, rows] - state[h]["peak"][c // own_chunks])
            s_s[h, rows] = e
            low = e.astype(BF16)
            p_s[h, rows] = low
            total += jnp.sum(e, axis=0, keepdims=True)
            mean += jnp.sum(e * ts_s[h, rows], axis=0, keepdims=True)
            acc += dot(vvT_s[2 * HD * h : 2 * HD * (h + 1), rows], low)
        inverse = 1.0 / total
        state[h].update(inverse=inverse, mean=mean * inverse, acc=acc)

    def tangent_pass(h):
        acc = 0.0
        for c in range(chunks):
            rows = pl.ds(c * kb, kb)
            low = (s_s[h, rows] * (ts_s[h, rows] - state[h]["mean"])).astype(BF16)
            acc += dot(vvT_s[2 * HD * h : 2 * HD * h + HD, rows], low)
        inverse, out = state[h]["inverse"], state[h]["acc"]
        residual = 2.0 * ((out[:HD] - out[HD:] - acc) * inverse - goal_t[HD * h : HD * h + HD])
        residual = residual * inverse
        zeros = jnp.zeros_like(residual)
        padded = jnp.concatenate((residual, zeros) if h == 0 else (zeros, residual), axis=0)
        state[h].update(r_t=padded.astype(BF16), r=padded.T.astype(BF16))

    def grad_pass(h):
        delta = 0.0
        for c in range(chunks):
            rows = pl.ds(c * kb, kb)
            grad = dot(v_s[rows], state[h]["r_t"])
            ts_s[h, rows] = grad
            delta += jnp.sum(s_s[h, rows] * grad, axis=0, keepdims=True)
            dv_s[rows] += dot(p_s[h, rows], state[h]["r"])
        state[h].update(delta=delta * state[h]["inverse"])

    def key_pass(h):
        acc = 0.0
        for c in range(chunks):
            rows = pl.ds(c * kb, kb)
            low = (s_s[h, rows] * (ts_s[h, rows] - state[h]["delta"])).astype(BF16)
            acc += dot(kT_s[HD * h : HD * h + HD, rows], low)
            dk_s[rows] += dot(low, state[h]["q"])
        dq_parts.append(acc)

    for stage in (score_pass, weight_pass, tangent_pass, grad_pass, key_pass):
        for h in range(2):
            stage(h)
    dq_s[qrows] = (jnp.concatenate(dq_parts, axis=0) * scale).T.astype(BF16)

    @pl.when(step == pl.num_programs(0) - 1)
    def _():
        dq_mine[...] = dq_s[:half]
        dq_part[...] = dq_s[half:]
        for i, grad in enumerate((dk_s, dv_s)):
            for part in range(2):
                own_out[part, i] = grad[part * half : (part + 1) * half]
                back_out[part, i] = grad[slab + part * half : slab + (part + 1) * half].astype(BF16)


def shape_of(shape, dtype):
    return jax.ShapeDtypeStruct(shape, dtype)


def core_pack(sources, chunks):
    rows = sources[0].shape[0]
    anywhere = pl.BlockSpec(memory_space=pl.ANY)
    return pl.pallas_call(
        functools.partial(core_pack_kernel, chunks),
        in_specs=[anywhere] * 6,
        out_specs=[anywhere] * chunks,
        out_shape=[shape_of((2, 6, rows, LANES), BF16)] * chunks,
        scratch_shapes=[pltpu.SemaphoreType.DMA((12 * chunks,))],
        name="core_pack",
    )(*sources)


def frame_pack(sources, target, got, chunk):
    rows = target.shape[0]
    anywhere = pl.BlockSpec(memory_space=pl.ANY)
    return pl.pallas_call(
        functools.partial(frame_pack_kernel, chunk),
        in_specs=[anywhere] * 8,
        out_specs=[anywhere] * 4,
        out_shape=[shape_of((4, rows, LANES), BF16)] * 2 + [shape_of((3, rows, LANES), BF16)] * 2,
        scratch_shapes=[pltpu.SemaphoreType.DMA((26,))],
        name="frame_pack",
    )(*sources, target, got)


def attend(flag, blocks, qb=256, kb=256):
    half = blocks[0].shape[1]
    slab = 2 * half

    def whole(shape):
        return pl.BlockSpec(shape, lambda i: (0,) * len(shape))

    outs = [
        shape_of((half, LANES), BF16),
        shape_of((half, LANES), BF16),
        shape_of((2, 2, half, LANES), F32),
        shape_of((2, 2, half, LANES), BF16),
    ]
    return pl.pallas_call(
        functools.partial(attend_kernel, qb, kb),
        grid=(slab // qb,),
        in_specs=[pl.BlockSpec(memory_space=pltpu.SMEM)] + [whole(b.shape) for b in blocks],
        out_specs=[whole(o.shape) for o in outs],
        out_shape=outs,
        scratch_shapes=[
            pltpu.VMEM((3, slab, LANES), BF16),
            pltpu.VMEM((2 * slab, LANES), BF16),
            pltpu.VMEM((2 * slab, 2 * LANES), BF16),
            pltpu.VMEM((LANES, 2 * slab), BF16),
            pltpu.VMEM((2 * LANES, 2 * slab), BF16),
            pltpu.VMEM((2, 2 * slab, qb), F32),
            pltpu.VMEM((2, 2 * slab, qb), F32),
            pltpu.VMEM((2, 2 * slab, qb), BF16),
            pltpu.VMEM((slab, LANES), BF16),
            pltpu.VMEM((2 * slab, LANES), F32),
            pltpu.VMEM((2 * slab, LANES), F32),
        ],
        compiler_params=pltpu.CompilerParams(vmem_limit_bytes=40 * 2**20),
        name="attend",
    )(flag, *blocks)


def on_device(query_main, key_main, value_main, query_tangent, key_tangent, value_tangent, target):
    sources = (key_main, value_main, key_tangent, value_tangent, query_main, query_tangent)
    half, columns = target.shape
    quarter = columns // 2
    chunks = quarter // LANES
    span = SLAB // half
    frames = lax.axis_size("frames")
    frame = lax.axis_index("frames")
    parity = frame % span
    flag = (frame >= span).astype(jnp.int32).reshape(1)
    swap = [(i, i ^ 1) for i in range(frames)]
    onward = [(i, i + span) for i in range(frames - span)]
    backward = [(b, a) for a, b in onward]

    sends = core_pack(sources, chunks)
    outs = [jnp.zeros((half, columns), BF16) for _ in range(3)]

    def place(out, block, side, chunk):
        return lax.dynamic_update_slice(out, block, (0, side * quarter + chunk * LANES))

    for chunk in range(chunks):
        got = lax.ppermute(sends[chunk], "heads", [(0, 1), (1, 0)])
        kv_mine, kv_send, q_mine, q_send = frame_pack(sources, target, got, chunk)
        kz_mine = lax.ppermute(kv_mine, "frames", onward)
        kv_part = lax.ppermute(kv_send, "frames", swap)
        q_part = lax.ppermute(q_send, "frames", swap)
        kz_part = lax.ppermute(kv_part, "frames", onward)
        dq_mine, dq_part, own, back = attend(
            flag, (q_mine, q_part, kv_mine, kv_part, kz_mine, kz_part)
        )
        dq_got = lax.ppermute(dq_part, "frames", swap)
        later = lax.ppermute(back, "frames", backward)
        summed = (own + later.astype(F32)).astype(BF16)
        pair_got = lax.ppermute(summed[1], "frames", swap)
        local = (dq_mine, summed[0, 0], summed[0, 1])
        remote = (dq_got, pair_got[0], pair_got[1])
        for i in range(3):
            outs[i] = place(outs[i], local[i], parity, chunk)
            outs[i] = place(outs[i], remote[i], 1 - parity, chunk)
    return tuple(outs)


def solution(mesh):
    tokens = P(("groups", "frames", "heads"), None)
    blocks = P(("groups", "frames"), "heads")
    return jax.shard_map(
        on_device,
        mesh=mesh,
        in_specs=(tokens,) * 6 + (blocks,),
        out_specs=(blocks,) * 3,
        check_vma=False,
    )
```

```python
import functools
import math

import jax
import jax.numpy as jnp
from jax import lax
from jax.experimental import pallas as pl
from jax.experimental.pallas import tpu as pltpu
from jax.sharding import PartitionSpec as P

HD = 64
SLAB = 768
LANES = 128
BF16 = jnp.bfloat16
F32 = jnp.float32


def dot(left, right):
    return lax.dot_general(left, right, (((1,), (0,)), ((), ())), preferred_element_type=F32)


def dot_nt(left, right):
    return lax.dot_general(left, right, (((1,), (1,)), ((), ())), preferred_element_type=F32)


def column_pack_kernel(chunks, place_ref, *refs):
    del place_ref
    sources, outs = refs[:6], refs[6:]
    quarter = sources[0].shape[1] // 2
    for chunk in range(chunks):
        for side in range(2):
            offset = side * quarter + chunk * LANES
            for i, source in enumerate(sources):
                outs[chunk][side, i] = source[:, offset : offset + LANES]


def frame_pack_kernel(chunk, place_ref, own, got, target, kv_mine, kv_send, q_mine, q_send):
    core, parity = place_ref[0], place_ref[1]
    rows = own.shape[2]
    quarter = target.shape[1] // 2
    own_rows = pl.ds(pl.multiple_of(core * rows, rows), rows)
    other_rows = pl.ds(pl.multiple_of((1 - core) * rows, rows), rows)
    for send in range(2):
        side = 1 - parity if send else parity
        kv_out = kv_send if send else kv_mine
        q_out = q_send if send else q_mine
        for i in range(6):
            out, j = (kv_out, i) if i < 4 else (q_out, i - 4)
            out[j, own_rows] = own[side, i]
            out[j, other_rows] = got[side, i]
        column = pl.multiple_of(side * quarter + chunk * LANES, LANES)
        q_out[2] = target[:, pl.ds(column, LANES)]


def attend_kernel(
    qb, kb, flag_ref,
    q_mine, q_part, kv_mine, kv_part, kz_mine, kz_part,
    dq_mine, dq_part, own_out, back_out,
    q_s, v_s, kkt_s, kT_s, vvT_s, s_s, ts_s, p_s, dq_s, dk_s, dv_s,
):
    half = q_mine.shape[1]
    slab = 2 * half
    own_chunks = slab // kb
    chunks = 2 * own_chunks
    step = pl.program_id(0)
    scale = 1.0 / math.sqrt(HD)

    @pl.when(step == 0)
    def _():
        for part, source in enumerate((q_mine, q_part)):
            rows = pl.ds(part * half, half)
            q_s[0, rows] = source[0] * jnp.asarray(scale, BF16)
            q_s[1, rows] = source[1] * jnp.asarray(scale, BF16)
            q_s[2, rows] = source[2]
        for part, source in enumerate((kv_mine, kv_part, kz_mine, kz_part)):
            rows = pl.ds(part * half, half)
            kkt_s[rows, :LANES] = source[0]
            kkt_s[rows, LANES:] = source[2]
            v_s[rows] = source[1]
            kT_s[:, rows] = source[0].T
            value_t = source[1].T
            vtangent_t = source[3].T
            for h in range(2):
                vvT_s[2 * HD * h : 2 * HD * h + HD, rows] = value_t[HD * h : HD * h + HD]
                vvT_s[2 * HD * h + HD : 2 * HD * (h + 1), rows] = vtangent_t[HD * h : HD * h + HD]
        dk_s[...] = jnp.zeros_like(dk_s)
        dv_s[...] = jnp.zeros_like(dv_s)

    lane = lax.broadcasted_iota(jnp.int32, (qb, LANES), 1)
    hide = (1.0 - flag_ref[0].astype(F32)) * 1e30
    qrows = pl.ds(pl.multiple_of(step * qb, qb), qb)
    queries = q_s[0, qrows]
    qtangent = q_s[1, qrows]
    goal_t = q_s[2, qrows].astype(F32).T
    state = [{}, {}]
    dq_parts = []

    def score_pass(h):
        keep = (lane // HD) == h
        q_masked = jnp.where(keep, queries, jnp.zeros_like(queries))
        qt_masked = jnp.where(keep, qtangent, jnp.zeros_like(qtangent))
        both = jnp.concatenate((qt_masked, q_masked), axis=1)
        peaks = [None, None]
        for c in range(chunks):
            rows = pl.ds(c * kb, kb)
            scores = dot_nt(kkt_s[rows, :LANES], q_masked)
            s_s[h, rows] = scores
            ts_s[h, rows] = dot_nt(kkt_s[rows], both)
            peak = jnp.max(scores, axis=0, keepdims=True)
            e = c // own_chunks
            peaks[e] = peak if peaks[e] is None else jnp.maximum(peaks[e], peak)
        peak = jnp.maximum(peaks[0], peaks[1] - hide)
        state[h].update(q=q_masked, peak=(peak, peak + hide))

    def weight_pass(h):
        total = mean = acc = 0.0
        for c in range(chunks):
            rows = pl.ds(c * kb, kb)
            e = jnp.exp(s_s[h, rows] - state[h]["peak"][c // own_chunks])
            s_s[h, rows] = e
            low = e.astype(BF16)
            p_s[h, rows] = low
            total += jnp.sum(e, axis=0, keepdims=True)
            mean += jnp.sum(e * ts_s[h, rows], axis=0, keepdims=True)
            acc += dot(vvT_s[2 * HD * h : 2 * HD * (h + 1), rows], low)
        inverse = 1.0 / total
        state[h].update(inverse=inverse, mean=mean * inverse, acc=acc)

    def tangent_pass(h):
        acc = 0.0
        for c in range(chunks):
            rows = pl.ds(c * kb, kb)
            low = (s_s[h, rows] * (ts_s[h, rows] - state[h]["mean"])).astype(BF16)
            acc += dot(vvT_s[2 * HD * h : 2 * HD * h + HD, rows], low)
        inverse, out = state[h]["inverse"], state[h]["acc"]
        residual = 2.0 * ((out[:HD] - out[HD:] - acc) * inverse - goal_t[HD * h : HD * h + HD])
        residual = residual * inverse
        zeros = jnp.zeros_like(residual)
        padded = jnp.concatenate((residual, zeros) if h == 0 else (zeros, residual), axis=0)
        state[h].update(r_t=padded.astype(BF16), r=padded.T.astype(BF16))

    def grad_pass(h):
        delta = 0.0
        for c in range(chunks):
            rows = pl.ds(c * kb, kb)
            grad = dot(v_s[rows], state[h]["r_t"])
            ts_s[h, rows] = grad
            delta += jnp.sum(s_s[h, rows] * grad, axis=0, keepdims=True)
            dv_s[rows] += dot(p_s[h, rows], state[h]["r"])
        state[h].update(delta=delta * state[h]["inverse"])

    def key_pass(h):
        acc = 0.0
        for c in range(chunks):
            rows = pl.ds(c * kb, kb)
            low = (s_s[h, rows] * (ts_s[h, rows] - state[h]["delta"])).astype(BF16)
            acc += dot(kT_s[HD * h : HD * h + HD, rows], low)
            dk_s[rows] += dot(low, state[h]["q"])
        dq_parts.append(acc)

    for stage in (score_pass, weight_pass, tangent_pass, grad_pass, key_pass):
        for h in range(2):
            stage(h)
    dq_s[qrows] = (jnp.concatenate(dq_parts, axis=0) * scale).T.astype(BF16)

    @pl.when(step == pl.num_programs(0) - 1)
    def _():
        dq_mine[...] = dq_s[:half]
        dq_part[...] = dq_s[half:]
        for i, grad in enumerate((dk_s, dv_s)):
            for part in range(2):
                own_out[part, i] = grad[part * half : (part + 1) * half]
                back_out[part, i] = grad[slab + part * half : slab + (part + 1) * half].astype(BF16)


def shape_of(shape, dtype):
    return jax.ShapeDtypeStruct(shape, dtype)


def column_pack(place, sources, chunks, flip):
    rows, columns = sources[0].shape
    half = pl.BlockSpec((rows, columns // 2), lambda i, p: (0, 1 - p[0] if flip else p[0]))
    outs = [shape_of((2, 6, rows, LANES), BF16)] * chunks
    return pl.pallas_call(
        functools.partial(column_pack_kernel, chunks),
        grid_spec=pltpu.PrefetchScalarGridSpec(
            num_scalar_prefetch=1,
            grid=(1,),
            in_specs=[half] * 6,
            out_specs=[pl.BlockSpec(o.shape, lambda i, p: (0,) * 4) for o in outs],
        ),
        out_shape=outs,
        name="column_pack",
    )(place, *sources)


def frame_pack(place, own, got, target, chunk):
    rows = target.shape[0]
    vmem = pl.BlockSpec(memory_space=pltpu.VMEM)
    return pl.pallas_call(
        functools.partial(frame_pack_kernel, chunk),
        in_specs=[pl.BlockSpec(memory_space=pltpu.SMEM)] + [vmem] * 3,
        out_specs=[vmem] * 4,
        out_shape=[shape_of((4, rows, LANES), BF16)] * 2 + [shape_of((3, rows, LANES), BF16)] * 2,
        name="frame_pack",
    )(place, own, got, target)


def attend(flag, blocks, qb=256, kb=256):
    half = blocks[0].shape[1]
    slab = 2 * half

    def whole(shape):
        return pl.BlockSpec(shape, lambda i: (0,) * len(shape))

    outs = [
        shape_of((half, LANES), BF16),
        shape_of((half, LANES), BF16),
        shape_of((2, 2, half, LANES), F32),
        shape_of((2, 2, half, LANES), BF16),
    ]
    return pl.pallas_call(
        functools.partial(attend_kernel, qb, kb),
        grid=(slab // qb,),
        in_specs=[pl.BlockSpec(memory_space=pltpu.SMEM)] + [whole(b.shape) for b in blocks],
        out_specs=[whole(o.shape) for o in outs],
        out_shape=outs,
        scratch_shapes=[
            pltpu.VMEM((3, slab, LANES), BF16),
            pltpu.VMEM((2 * slab, LANES), BF16),
            pltpu.VMEM((2 * slab, 2 * LANES), BF16),
            pltpu.VMEM((LANES, 2 * slab), BF16),
            pltpu.VMEM((2 * LANES, 2 * slab), BF16),
            pltpu.VMEM((2, 2 * slab, qb), F32),
            pltpu.VMEM((2, 2 * slab, qb), F32),
            pltpu.VMEM((2, 2 * slab, qb), BF16),
            pltpu.VMEM((slab, LANES), BF16),
            pltpu.VMEM((2 * slab, LANES), F32),
            pltpu.VMEM((2 * slab, LANES), F32),
        ],
        compiler_params=pltpu.CompilerParams(vmem_limit_bytes=40 * 2**20),
        name="attend",
    )(flag, *blocks)


def on_device(query_main, key_main, value_main, query_tangent, key_tangent, value_tangent, target):
    sources = (key_main, value_main, key_tangent, value_tangent, query_main, query_tangent)
    half, columns = target.shape
    quarter = columns // 2
    chunks = quarter // LANES
    span = SLAB // half
    frames = lax.axis_size("frames")
    frame = lax.axis_index("frames")
    parity = frame % span
    flag = (frame >= span).astype(jnp.int32).reshape(1)
    swap = [(i, i ^ 1) for i in range(frames)]
    onward = [(i, i + span) for i in range(frames - span)]
    backward = [(b, a) for a, b in onward]

    place_ids = jnp.stack((lax.axis_index("heads"), parity)).astype(jnp.int32)
    sends = column_pack(place_ids, sources, chunks, True)
    keeps = column_pack(place_ids, sources, chunks, False)
    outs = [jnp.zeros((half, columns), BF16) for _ in range(3)]

    def place(out, block, side, chunk):
        return lax.dynamic_update_slice(out, block, (0, side * quarter + chunk * LANES))

    for chunk in range(chunks):
        got = lax.ppermute(sends[chunk], "heads", [(0, 1), (1, 0)])
        kv_mine, kv_send, q_mine, q_send = frame_pack(place_ids, keeps[chunk], got, target, chunk)
        kz_mine = lax.ppermute(kv_mine, "frames", onward)
        kv_part = lax.ppermute(kv_send, "frames", swap)
        q_part = lax.ppermute(q_send, "frames", swap)
        kz_part = lax.ppermute(kv_part, "frames", onward)
        dq_mine, dq_part, own, back = attend(
            flag, (q_mine, q_part, kv_mine, kv_part, kz_mine, kz_part)
        )
        dq_got = lax.ppermute(dq_part, "frames", swap)
        later = lax.ppermute(back, "frames", backward)
        summed = (own + later.astype(F32)).astype(BF16)
        pair_got = lax.ppermute(summed[1], "frames", swap)
        local = (dq_mine, summed[0, 0], summed[0, 1])
        remote = (dq_got, pair_got[0], pair_got[1])
        for i in range(3):
            outs[i] = place(outs[i], local[i], parity, chunk)
            outs[i] = place(outs[i], remote[i], 1 - parity, chunk)
    return tuple(outs)


def solution(mesh):
    tokens = P(("groups", "frames", "heads"), None)
    blocks = P(("groups", "frames"), "heads")
    return jax.shard_map(
        on_device,
        mesh=mesh,
        in_specs=(tokens,) * 6 + (blocks,),
        out_specs=(blocks,) * 3,
        check_vma=False,
    )
```

```python
import functools
import math

import jax
import jax.numpy as jnp
from jax import lax
from jax.experimental import pallas as pl
from jax.experimental.pallas import tpu as pltpu
from jax.sharding import PartitionSpec as P


HD = 64
SLAB = 768
LANES = 128
BF16 = jnp.bfloat16
F32 = jnp.float32


def dot(left, right):
    return lax.dot_general(left, right, (((1,), (0,)), ((), ())), preferred_element_type=F32)


def dot_nt(left, right):
    return lax.dot_general(left, right, (((1,), (1,)), ((), ())), preferred_element_type=F32)


def column_pack_kernel(chunks, place_ref, *refs):
    del place_ref
    sources, outs = refs[:6], refs[6:]
    quarter = sources[0].shape[1] // 2
    for chunk in range(chunks):
        for side in range(2):
            offset = side * quarter + chunk * LANES
            for i, source in enumerate(sources):
                outs[chunk][side, i] = source[:, offset : offset + LANES]


def frame_pack_kernel(chunk, place_ref, own, got, target, kv_mine, kv_send, q_mine, q_send):
    core, parity = place_ref[0], place_ref[1]
    rows = own.shape[2]
    quarter = target.shape[1] // 2
    own_rows = pl.ds(pl.multiple_of(core * rows, rows), rows)
    other_rows = pl.ds(pl.multiple_of((1 - core) * rows, rows), rows)
    for send in range(2):
        side = 1 - parity if send else parity
        kv_out = kv_send if send else kv_mine
        q_out = q_send if send else q_mine
        for i in range(6):
            out, j = (kv_out, i) if i < 4 else (q_out, i - 4)
            out[j, own_rows] = own[side, i]
            out[j, other_rows] = got[side, i]
        column = pl.multiple_of(side * quarter + chunk * LANES, LANES)
        q_out[2] = target[:, pl.ds(column, LANES)]


def attend_kernel(
    qb, kb, flag_ref,
    q_mine, q_part, kv_mine, kv_part, kz_mine, kz_part,
    dq_mine, own_mine, back_mine, ret_part, back_part,
    q_s, v_s, kkt_s, kT_s, vvT_s, s_s, ts_s, p_s, dq_s, dk_s, dv_s,
):
    half = q_mine.shape[1]
    slab = 2 * half
    own_chunks = slab // kb
    chunks = 2 * own_chunks
    step = pl.program_id(0)
    scale = 1.0 / math.sqrt(HD)

    @pl.when(step == 0)
    def _():
        for part, source in enumerate((q_mine, q_part)):
            rows = pl.ds(part * half, half)
            q_s[0, rows] = source[0] * jnp.asarray(scale, BF16)
            q_s[1, rows] = source[1] * jnp.asarray(scale, BF16)
            q_s[2, rows] = source[2]
        for part, source in enumerate((kv_mine, kv_part, kz_mine, kz_part)):
            rows = pl.ds(part * half, half)
            kkt_s[rows, :LANES] = source[0]
            kkt_s[rows, LANES:] = source[2]
            v_s[rows] = source[1]
            kT_s[:, rows] = source[0].T
            value_t = source[1].T
            vtangent_t = source[3].T
            for h in range(2):
                vvT_s[2 * HD * h : 2 * HD * h + HD, rows] = value_t[HD * h : HD * h + HD]
                vvT_s[2 * HD * h + HD : 2 * HD * (h + 1), rows] = vtangent_t[HD * h : HD * h + HD]
        dk_s[...] = jnp.zeros_like(dk_s)
        dv_s[...] = jnp.zeros_like(dv_s)

    lane = lax.broadcasted_iota(jnp.int32, (qb, LANES), 1)
    hide = (1.0 - flag_ref[0].astype(F32)) * 1e30
    qrows = pl.ds(pl.multiple_of(step * qb, qb), qb)
    queries = q_s[0, qrows]
    qtangent = q_s[1, qrows]
    goal_t = q_s[2, qrows].astype(F32).T
    state = [{}, {}]
    dq_parts = []

    def score_pass(h):
        keep = (lane // HD) == h
        q_masked = jnp.where(keep, queries, jnp.zeros_like(queries))
        qt_masked = jnp.where(keep, qtangent, jnp.zeros_like(qtangent))
        both = jnp.concatenate((qt_masked, q_masked), axis=1)
        peaks = [None, None]
        for c in range(chunks):
            rows = pl.ds(c * kb, kb)
            scores = dot_nt(kkt_s[rows, :LANES], q_masked)
            s_s[h, rows] = scores
            ts_s[h, rows] = dot_nt(kkt_s[rows], both)
            peak = jnp.max(scores, axis=0, keepdims=True)
            e = c // own_chunks
            peaks[e] = peak if peaks[e] is None else jnp.maximum(peaks[e], peak)
        peak = jnp.maximum(peaks[0], peaks[1] - hide)
        state[h].update(q=q_masked, peak=(peak, peak + hide))

    def weight_pass(h):
        total = mean = acc = 0.0
        for c in range(chunks):
            rows = pl.ds(c * kb, kb)
            e = jnp.exp(s_s[h, rows] - state[h]["peak"][c // own_chunks])
            s_s[h, rows] = e
            low = e.astype(BF16)
            p_s[h, rows] = low
            total += jnp.sum(e, axis=0, keepdims=True)
            mean += jnp.sum(e * ts_s[h, rows], axis=0, keepdims=True)
            acc += dot(vvT_s[2 * HD * h : 2 * HD * (h + 1), rows], low)
        inverse = 1.0 / total
        state[h].update(inverse=inverse, mean=mean * inverse, acc=acc)

    def tangent_pass(h):
        acc = 0.0
        for c in range(chunks):
            rows = pl.ds(c * kb, kb)
            low = (s_s[h, rows] * (ts_s[h, rows] - state[h]["mean"])).astype(BF16)
            acc += dot(vvT_s[2 * HD * h : 2 * HD * h + HD, rows], low)
        inverse, out = state[h]["inverse"], state[h]["acc"]
        residual = 2.0 * ((out[:HD] - out[HD:] - acc) * inverse - goal_t[HD * h : HD * h + HD])
        residual = residual * inverse
        zeros = jnp.zeros_like(residual)
        padded = jnp.concatenate((residual, zeros) if h == 0 else (zeros, residual), axis=0)
        state[h].update(r_t=padded.astype(BF16), r=padded.T.astype(BF16))

    def grad_pass(h):
        delta = 0.0
        for c in range(chunks):
            rows = pl.ds(c * kb, kb)
            grad = dot(v_s[rows], state[h]["r_t"])
            ts_s[h, rows] = grad
            delta += jnp.sum(s_s[h, rows] * grad, axis=0, keepdims=True)
            dv_s[rows] += dot(p_s[h, rows], state[h]["r"])
        state[h].update(delta=delta * state[h]["inverse"])

    def key_pass(h):
        acc = 0.0
        for c in range(chunks):
            rows = pl.ds(c * kb, kb)
            low = (s_s[h, rows] * (ts_s[h, rows] - state[h]["delta"])).astype(BF16)
            acc += dot(kT_s[HD * h : HD * h + HD, rows], low)
            dk_s[rows] += dot(low, state[h]["q"])
        dq_parts.append(acc)

    for stage in (score_pass, weight_pass, tangent_pass, grad_pass, key_pass):
        for h in range(2):
            stage(h)
    dq_s[qrows] = (jnp.concatenate(dq_parts, axis=0) * scale).T.astype(BF16)

    @pl.when(step == pl.num_programs(0) - 1)
    def _():
        dq_mine[...] = dq_s[:half]
        ret_part[0] = dq_s[half:]
        for i, grad in enumerate((dk_s, dv_s)):
            own_mine[i] = grad[:half]
            ret_part[i + 1] = grad[half:slab].astype(BF16)
            back_mine[i] = grad[slab : slab + half].astype(BF16)
            back_part[i] = grad[slab + half :].astype(BF16)


def shape_of(shape, dtype):
    return jax.ShapeDtypeStruct(shape, dtype)


def column_pack(place, sources, chunks, flip):
    rows, columns = sources[0].shape
    half = pl.BlockSpec((rows, columns // 2), lambda i, p: (0, 1 - p[0] if flip else p[0]))
    outs = [shape_of((2, 6, rows, LANES), BF16)] * chunks
    return pl.pallas_call(
        functools.partial(column_pack_kernel, chunks),
        grid_spec=pltpu.PrefetchScalarGridSpec(
            num_scalar_prefetch=1,
            grid=(1,),
            in_specs=[half] * 6,
            out_specs=[pl.BlockSpec(o.shape, lambda i, p: (0,) * 4) for o in outs],
        ),
        out_shape=outs,
        name="column_pack",
    )(place, *sources)


def frame_pack(place, own, got, target, chunk):
    rows = target.shape[0]
    vmem = pl.BlockSpec(memory_space=pltpu.VMEM)
    return pl.pallas_call(
        functools.partial(frame_pack_kernel, chunk),
        in_specs=[pl.BlockSpec(memory_space=pltpu.SMEM)] + [vmem] * 3,
        out_specs=[vmem] * 4,
        out_shape=[shape_of((4, rows, LANES), BF16)] * 2 + [shape_of((3, rows, LANES), BF16)] * 2,
        name="frame_pack",
    )(place, own, got, target)


def attend(flag, blocks, qb=256, kb=256):
    half = blocks[0].shape[1]
    slab = 2 * half

    def whole(shape):
        return pl.BlockSpec(shape, lambda i: (0,) * len(shape))

    outs = [
        shape_of((half, LANES), BF16),
        shape_of((2, half, LANES), F32),
        shape_of((2, half, LANES), BF16),
        shape_of((3, half, LANES), BF16),
        shape_of((2, half, LANES), BF16),
    ]
    return pl.pallas_call(
        functools.partial(attend_kernel, qb, kb),
        grid=(slab // qb,),
        in_specs=[pl.BlockSpec(memory_space=pltpu.SMEM)] + [whole(b.shape) for b in blocks],
        out_specs=[whole(o.shape) for o in outs],
        out_shape=outs,
        scratch_shapes=[
            pltpu.VMEM((3, slab, LANES), BF16),
            pltpu.VMEM((2 * slab, LANES), BF16),
            pltpu.VMEM((2 * slab, 2 * LANES), BF16),
            pltpu.VMEM((LANES, 2 * slab), BF16),
            pltpu.VMEM((2 * LANES, 2 * slab), BF16),
            pltpu.VMEM((2, 2 * slab, qb), F32),
            pltpu.VMEM((2, 2 * slab, qb), F32),
            pltpu.VMEM((2, 2 * slab, qb), BF16),
            pltpu.VMEM((slab, LANES), BF16),
            pltpu.VMEM((2 * slab, LANES), F32),
            pltpu.VMEM((2 * slab, LANES), F32),
        ],
        compiler_params=pltpu.CompilerParams(vmem_limit_bytes=40 * 2**20),
        name="attend",
    )(flag, *blocks)


def on_device(query_main, key_main, value_main, query_tangent, key_tangent, value_tangent, target):
    sources = (key_main, value_main, key_tangent, value_tangent, query_main, query_tangent)
    half, columns = target.shape
    quarter = columns // 2
    chunks = quarter // LANES
    span = SLAB // half
    frames = lax.axis_size("frames")
    frame = lax.axis_index("frames")
    parity = frame % span
    flag = (frame >= span).astype(jnp.int32).reshape(1)
    swap = [(i, i ^ 1) for i in range(frames)]
    onward = [(i, i + span) for i in range(frames - span)]
    backward = [(b, a) for a, b in onward]
    across = [(b, a ^ 1) for a, b in onward]
    place_ids = jnp.stack((lax.axis_index("heads"), parity)).astype(jnp.int32)

    sends = column_pack(place_ids, sources, chunks, True)
    keeps = column_pack(place_ids, sources, chunks, False)
    moved = []
    for n in range(chunks):
        got = lax.ppermute(sends[n], "heads", [(0, 1), (1, 0)])
        kv_mine, kv_send, q_mine, q_send = frame_pack(place_ids, keeps[n], got, target, n)
        kz_mine = lax.ppermute(kv_mine, "frames", onward)
        kv_part = lax.ppermute(kv_send, "frames", swap)
        q_part = lax.ppermute(q_send, "frames", swap)
        kz_part = lax.ppermute(kv_part, "frames", onward)
        moved.append((q_mine, q_part, kv_mine, kv_part, kz_mine, kz_part))
    outs = [jnp.zeros((half, columns), BF16) for _ in range(3)]

    def put(out, block, side, n):
        return lax.dynamic_update_slice(out, block, (0, side * quarter + n * LANES))

    for n in range(chunks):
        dq_mine, own_mine, back_mine, ret_part, back_part = attend(flag, moved[n])
        later = lax.ppermute(back_mine, "frames", backward)
        later_part = lax.ppermute(back_part, "frames", across)
        ret = lax.ppermute(ret_part, "frames", swap)
        mine = (own_mine + later.astype(F32)).astype(BF16)
        part = (ret[1:].astype(F32) + later_part.astype(F32)).astype(BF16)
        local = (dq_mine, mine[0], mine[1])
        remote = (ret[0], part[0], part[1])
        for i in range(3):
            outs[i] = put(outs[i], local[i], parity, n)
            outs[i] = put(outs[i], remote[i], 1 - parity, n)
    return tuple(outs)


def solution(mesh):
    tokens = P(("groups", "frames", "heads"), None)
    blocks = P(("groups", "frames"), "heads")
    return jax.shard_map(
        on_device,
        mesh=mesh,
        in_specs=(tokens,) * 6 + (blocks,),
        out_specs=(blocks,) * 3,
        check_vma=False,
    )
```

```python
import functools
import math

import jax
import jax.numpy as jnp
from jax import lax
from jax.experimental import pallas as pl
from jax.experimental.pallas import tpu as pltpu
from jax.sharding import PartitionSpec as P


HD = 64
SLAB = 768
LANES = 128
BF16 = jnp.bfloat16
F32 = jnp.float32


def dot(left, right):
    return lax.dot_general(left, right, (((1,), (0,)), ((), ())), preferred_element_type=F32)


def dot_nt(left, right):
    return lax.dot_general(left, right, (((1,), (1,)), ((), ())), preferred_element_type=F32)


def block_pack_kernel(*refs):
    place_ref, refs = refs[0], refs[1:]
    sources, goals, outs = refs[:24], refs[24:26], refs[26:]
    zk, ykv, yq, oq, cross = outs
    core = place_ref[0]
    rows = zk.shape[2]
    for i in range(6):
        mine, part = sources[4 * i : 4 * i + 2], sources[4 * i + 2 : 4 * i + 4]
        for c in range(2):
            if i < 4:
                zk[c, i] = mine[c][...]
                ykv[c, i] = part[c][...]
            else:
                yq[c, i - 4] = part[c][...]

            @pl.when(core == c)
            def _():
                cross[0, i] = mine[1 - c][...]
                if i >= 4:
                    oq[i - 4] = mine[c][...]

    for c in range(2):
        yq[c, 2] = goals[1][c * rows : (c + 1) * rows]
        oq[2 + c] = goals[0][c * rows : (c + 1) * rows]


def rest_pack_kernel(first, place_ref, *refs):
    sources, target, outs, cross = refs[:6], refs[6], refs[7:-1], refs[-1]
    core, parity = place_ref[0], place_ref[1]
    rows, width = sources[0].shape
    half = width // 2
    quarter = half // 2

    def columns(c, side, n):
        return pl.ds(pl.multiple_of(c * half + side * quarter + n * LANES, LANES), LANES)

    for k in range(len(outs) // 4):
        zk, ykv, yq, oq = outs[4 * k : 4 * k + 4]
        n = first + k
        for c in range(2):
            for i in range(4):
                zk[c, i] = sources[i][:, columns(c, parity, n)]
                ykv[c, i] = sources[i][:, columns(c, 1 - parity, n)]
            for i in range(2):
                yq[c, i] = sources[4 + i][:, columns(c, 1 - parity, n)]
            block = slice(c * rows, (c + 1) * rows)
            yq[c, 2] = target[block, columns(0, 1 - parity, n)]
            oq[2 + c] = target[block, columns(0, parity, n)]
        for i in range(2):
            oq[i] = sources[4 + i][:, columns(core, parity, n)]
        for i in range(6):
            cross[k, i] = sources[i][:, columns(1 - core, parity, n)]


def attend_kernel(qb, kb, held, place_ref, *refs):
    oq, cross, zk, ykv, ykv_x, yq, yq_x, zown, zown_x, zpart, zpart_x = refs[:11]
    dq_mine, own_mine, back_mine, ret_part, back_part = refs[11 + held : 16 + held]
    q_s, v_s, kkt_s, kT_s, vvT_s, s_s, ts_s, p_s, dq_s, dk_s, dv_s = refs[16 + held :]
    rows_each = zk.shape[1]
    half = 2 * rows_each
    slab = 2 * half
    own_chunks = slab // kb
    chunks = 2 * own_chunks
    step = pl.program_id(0)
    core = place_ref[0]
    scale = 1.0 / math.sqrt(HD)

    @pl.when(step == 0)
    def _():
        queries = ((oq[0], oq[1], oq[2 + core]), (cross[4], cross[5], oq[3 - core]))
        queries += ((yq[core, 0], yq[core, 1], yq[core, 2]),)
        queries += ((yq_x[0], yq_x[1], yq[1 - core, 2]),)
        for part, (query, tangent, goal) in enumerate(queries):
            rows = pl.ds(part * rows_each, rows_each)
            q_s[0, rows] = query * jnp.asarray(scale, BF16)
            q_s[1, rows] = tangent * jnp.asarray(scale, BF16)
            q_s[2, rows] = goal
        for part, source in enumerate((zk, cross, ykv, ykv_x, zown, zown_x, zpart, zpart_x)):
            rows = pl.ds(part * rows_each, rows_each)
            kkt_s[rows, :LANES] = source[0]
            kkt_s[rows, LANES:] = source[2]
            v_s[rows] = source[1]
        for part in range(4):
            rows = pl.ds(part * half, half)
            kT_s[:, rows] = kkt_s[rows, :LANES].T
            value_t = v_s[rows].T
            sources = ((zk, cross), (ykv, ykv_x), (zown, zown_x), (zpart, zpart_x))[part]
            vtangent_t = jnp.concatenate((sources[0][3], sources[1][3]), axis=0).T
            for h in range(2):
                vvT_s[2 * HD * h : 2 * HD * h + HD, rows] = value_t[HD * h : HD * h + HD]
                vvT_s[2 * HD * h + HD : 2 * HD * (h + 1), rows] = vtangent_t[HD * h : HD * h + HD]
        dk_s[...] = jnp.zeros_like(dk_s)
        dv_s[...] = jnp.zeros_like(dv_s)

    lane = lax.broadcasted_iota(jnp.int32, (qb, LANES), 1)
    hide = (1.0 - place_ref[2].astype(F32)) * 1e30
    qrows = pl.ds(pl.multiple_of(step * qb, qb), qb)
    queries = q_s[0, qrows]
    qtangent = q_s[1, qrows]
    goal_t = q_s[2, qrows].astype(F32).T
    state = [{}, {}]
    dq_parts = []

    def score_pass(h):
        keep = (lane // HD) == h
        q_masked = jnp.where(keep, queries, jnp.zeros_like(queries))
        qt_masked = jnp.where(keep, qtangent, jnp.zeros_like(qtangent))
        both = jnp.concatenate((qt_masked, q_masked), axis=1)
        peaks = [None, None]
        for c in range(chunks):
            rows = pl.ds(c * kb, kb)
            scores = dot_nt(kkt_s[rows, :LANES], q_masked)
            s_s[h, rows] = scores
            ts_s[h, rows] = dot_nt(kkt_s[rows], both)
            peak = jnp.max(scores, axis=0, keepdims=True)
            e = c // own_chunks
            peaks[e] = peak if peaks[e] is None else jnp.maximum(peaks[e], peak)
        peak = jnp.maximum(peaks[0], peaks[1] - hide)
        state[h].update(q=q_masked, peak=(peak, peak + hide))

    def weight_pass(h):
        total = mean = acc = 0.0
        for c in range(chunks):
            rows = pl.ds(c * kb, kb)
            e = jnp.exp(s_s[h, rows] - state[h]["peak"][c // own_chunks])
            s_s[h, rows] = e
            low = e.astype(BF16)
            p_s[h, rows] = low
            total += jnp.sum(e, axis=0, keepdims=True)
            mean += jnp.sum(e * ts_s[h, rows], axis=0, keepdims=True)
            acc += dot(vvT_s[2 * HD * h : 2 * HD * (h + 1), rows], low)
        inverse = 1.0 / total
        state[h].update(inverse=inverse, mean=mean * inverse, acc=acc)

    def tangent_pass(h):
        acc = 0.0
        for c in range(chunks):
            rows = pl.ds(c * kb, kb)
            low = (s_s[h, rows] * (ts_s[h, rows] - state[h]["mean"])).astype(BF16)
            acc += dot(vvT_s[2 * HD * h : 2 * HD * h + HD, rows], low)
        inverse, out = state[h]["inverse"], state[h]["acc"]
        residual = 2.0 * ((out[:HD] - out[HD:] - acc) * inverse - goal_t[HD * h : HD * h + HD])
        residual = residual * inverse
        zeros = jnp.zeros_like(residual)
        padded = jnp.concatenate((residual, zeros) if h == 0 else (zeros, residual), axis=0)
        state[h].update(r_t=padded.astype(BF16), r=padded.T.astype(BF16))

    def grad_pass(h):
        delta = 0.0
        for c in range(chunks):
            rows = pl.ds(c * kb, kb)
            grad = dot(v_s[rows], state[h]["r_t"])
            ts_s[h, rows] = grad
            delta += jnp.sum(s_s[h, rows] * grad, axis=0, keepdims=True)
            dv_s[rows] += dot(p_s[h, rows], state[h]["r"])
        state[h].update(delta=delta * state[h]["inverse"])

    def key_pass(h):
        acc = 0.0
        for c in range(chunks):
            rows = pl.ds(c * kb, kb)
            low = (s_s[h, rows] * (ts_s[h, rows] - state[h]["delta"])).astype(BF16)
            acc += dot(kT_s[HD * h : HD * h + HD, rows], low)
            dk_s[rows] += dot(low, state[h]["q"])
        dq_parts.append(acc)

    for stage in (score_pass, weight_pass, tangent_pass, grad_pass, key_pass):
        for h in range(2):
            stage(h)
    dq_s[qrows] = (jnp.concatenate(dq_parts, axis=0) * scale).T.astype(BF16)

    @pl.when(step == pl.num_programs(0) - 1)
    def _():
        for block in range(2):
            place = pl.multiple_of((core if block == 0 else 1 - core) * rows_each, rows_each)
            rows = pl.ds(place, rows_each)
            mine = slice(block * rows_each, (block + 1) * rows_each)
            part = slice(half + block * rows_each, half + (block + 1) * rows_each)
            dq_mine[rows] = dq_s[mine]
            ret_part[0, rows] = dq_s[part]
            for i, grad in enumerate((dk_s, dv_s)):
                own_mine[i, rows] = grad[mine]
                ret_part[i + 1, rows] = grad[part].astype(BF16)
                early = grad[slab : 2 * slab]
                back_mine[i, rows] = early[mine].astype(BF16)
                back_part[i, rows] = early[part].astype(BF16)


def shape_of(shape, dtype):
    return jax.ShapeDtypeStruct(shape, dtype)


def chunk_shapes(rows):
    return [
        shape_of((2, 4, rows, LANES), BF16),
        shape_of((2, 4, rows, LANES), BF16),
        shape_of((2, 3, rows, LANES), BF16),
        shape_of((4, rows, LANES), BF16),
    ]


def whole(shape):
    return pl.BlockSpec(shape, lambda i, p: (0,) * len(shape))


def block_pack(place, sources, target, n):
    rows, width = sources[0].shape
    across = width // LANES // 2
    per_side = across // 2
    specs = []
    operands = []

    def column_spec(height, c, flip):
        def index(i, p):
            return (0, c * across + (1 - p[1] if flip else p[1]) * per_side + n)

        return pl.BlockSpec((height, LANES), index)

    for source in sources:
        for flip in (False, True):
            for c in range(2):
                specs.append(column_spec(rows, c, flip))
                operands.append(source)
    for flip in (False, True):
        specs.append(column_spec(target.shape[0], 0, flip))
        operands.append(target)
    outs = chunk_shapes(rows) + [shape_of((1, 6, rows, LANES), BF16)]
    return pl.pallas_call(
        block_pack_kernel,
        grid_spec=pltpu.PrefetchScalarGridSpec(
            num_scalar_prefetch=1,
            grid=(1,),
            in_specs=specs,
            out_specs=[whole(o.shape) for o in outs],
        ),
        out_shape=outs,
        name="block_pack",
    )(place, *operands)


def rest_pack(place, sources, target, first, count):
    rows = sources[0].shape[0]
    operands = (*sources, target)
    outs = chunk_shapes(rows) * count + [shape_of((count, 6, rows, LANES), BF16)]
    return pl.pallas_call(
        functools.partial(rest_pack_kernel, first),
        grid_spec=pltpu.PrefetchScalarGridSpec(
            num_scalar_prefetch=1,
            grid=(1,),
            in_specs=[whole(o.shape) for o in operands],
            out_specs=[whole(o.shape) for o in outs],
        ),
        out_shape=outs,
        name="rest_pack",
    )(place, *operands)


def attend(place, blocks, cross_index, batch, index, previous, qb=256, kb=256):
    rows = blocks[0].shape[1]
    half = 2 * rows
    slab = 2 * half

    def slot(array):
        return pl.BlockSpec((None,) + array.shape[1:], lambda i, p: (p[0], 0, 0, 0))

    def single(shape, at):
        return pl.BlockSpec((None,) + shape[1:], lambda i, p: (at,) + (0,) * (len(shape) - 1))

    oq, cross, zk, ykv, ykv_x, yq, yq_x, *early = blocks
    in_specs = [whole(oq.shape), single(cross.shape, cross_index)]
    in_specs += [slot(zk), slot(ykv), slot(ykv_x), whole(yq.shape), slot(yq_x)]
    in_specs += [slot(b) for b in early]
    outs = [
        shape_of((batch, half, LANES), BF16),
        shape_of((batch, 2, half, LANES), F32),
        shape_of((batch, 2, half, LANES), BF16),
        shape_of((batch, 3, half, LANES), BF16),
        shape_of((batch, 2, half, LANES), BF16),
    ]
    held = () if previous is None else tuple(previous)
    in_specs += [pl.BlockSpec(memory_space=pl.ANY)] * len(held)
    return pl.pallas_call(
        functools.partial(attend_kernel, qb, kb, len(held)),
        grid_spec=pltpu.PrefetchScalarGridSpec(
            num_scalar_prefetch=1,
            grid=(slab // qb,),
            in_specs=in_specs,
            out_specs=[single(o.shape, index) for o in outs],
            scratch_shapes=[
                pltpu.VMEM((3, slab, LANES), BF16),
                pltpu.VMEM((2 * slab, LANES), BF16),
                pltpu.VMEM((2 * slab, 2 * LANES), BF16),
                pltpu.VMEM((LANES, 2 * slab), BF16),
                pltpu.VMEM((2 * LANES, 2 * slab), BF16),
                pltpu.VMEM((2, 2 * slab, qb), F32),
                pltpu.VMEM((2, 2 * slab, qb), F32),
                pltpu.VMEM((2, 2 * slab, qb), BF16),
                pltpu.VMEM((slab, LANES), BF16),
                pltpu.VMEM((2 * slab, LANES), F32),
                pltpu.VMEM((2 * slab, LANES), F32),
            ],
        ),
        out_shape=outs,
        input_output_aliases={1 + len(blocks) + i: i for i in range(len(held))},
        compiler_params=pltpu.CompilerParams(vmem_limit_bytes=40 * 2**20),
        name="attend",
    )(place, *blocks, *held)


def on_device(query_main, key_main, value_main, query_tangent, key_tangent, value_tangent, target):
    sources = (key_main, value_main, key_tangent, value_tangent, query_main, query_tangent)
    half, columns = target.shape
    quarter = columns // 2
    chunks = quarter // LANES
    span = SLAB // half
    frames = lax.axis_size("frames")
    frame = lax.axis_index("frames")
    parity = frame % span
    flag = frame >= span
    place = jnp.stack([x.astype(jnp.int32) for x in (lax.axis_index("heads"), parity, flag)])
    swap = [(i, i ^ 1) for i in range(frames)]
    onward = [(i, (i + span) % frames) for i in range(frames)]
    backward = [(b, a) for a, b in onward]
    across = [(b, a ^ 1) for a, b in onward]

    def send(array, route):
        return lax.ppermute(array, "frames", route)

    def trade(array):
        return lax.ppermute(array, "heads", [(0, 1), (1, 0)])

    *packed, cross0 = block_pack(place, sources, target, 0)
    *rest, cross1 = rest_pack(place, sources, target, 1, chunks - 1)
    packed += rest
    cross = [trade(cross0)] + [trade(cross1)] * (chunks - 1)
    moved = []
    for n in range(chunks):
        zk, ykv, yq, oq = packed[4 * n : 4 * n + 4]
        zown = send(zk, onward)
        kv = send(ykv, swap)
        zpart = send(kv, onward)
        q = send(yq, swap)
        moved.append(
            (oq, cross[n], zk, kv, trade(kv), q, trade(q))
            + (zown, trade(zown), zpart, trade(zpart))
        )
    outs = [jnp.zeros((half, columns), BF16) for _ in range(3)]

    def put(out, block, side, n):
        return lax.dynamic_update_slice(out, block, (0, side * quarter + n * LANES))

    batches = [list(range(chunks - 1)), [chunks - 1]]
    for batch in batches:
        grads = None
        for k, n in enumerate(batch):
            grads = attend(place, moved[n], max(n - 1, 0), len(batch), k, grads)
        dq_mine, own_mine, back_mine, ret_part, back_part = grads
        later = send(back_mine, backward)
        later_part = send(back_part, across)
        ret = send(ret_part, swap)
        mine = (own_mine + later.astype(F32)).astype(BF16)
        part = (ret[:, 1:].astype(F32) + later_part.astype(F32)).astype(BF16)
        for k, n in enumerate(batch):
            local = (dq_mine[k], mine[k, 0], mine[k, 1])
            remote = (ret[k, 0], part[k, 0], part[k, 1])
            for i in range(3):
                outs[i] = put(outs[i], local[i], parity, n)
                outs[i] = put(outs[i], remote[i], 1 - parity, n)
    return tuple(outs)


def solution(mesh):
    tokens = P(("groups", "frames", "heads"), None)
    blocks = P(("groups", "frames"), "heads")
    return jax.shard_map(
        on_device,
        mesh=mesh,
        in_specs=(tokens,) * 6 + (blocks,),
        out_specs=(blocks,) * 3,
        check_vma=False,
    )
```
